32 devices in a mesh: hst: 8 (over y, x, core), local: 4 (over z).
Axes of the slice: x: 2, y: 2, z: 4, core: 2. Of those that a mesh axis runs over, the one named last changes fastest.
Arguments:
- image_feats: bfloat16 [4096, 1152], P(('hst', 'local')), may hold values from -6 to 6
- text_feats: bfloat16 [4096, 1152], P(('hst', 'local')), may hold values from -6 to 6
- image_proj: bfloat16 [1152, 1152], replicated, may hold values from -0.1875 to 0.1875
- text_proj: bfloat16 [1152, 1152], replicated, may hold values from -0.1875 to 0.1875
- scale: float32 [1], replicated, may hold values from 4 to 16
- bias: float32 [1], replicated, may hold values from -4 to -2
Outputs:
- image_grad: float32 [4096, 1152], P(('hst', 'local'))
- text_grad: float32 [4096, 1152], P(('hst', 'local'))
The draws below stay inside these ranges and needn't reach their ends.
All inputs are finite; a program needn't handle non-finite values.
Results may differ from the reference program's by a relative error of at most 0.005.
Values may be sent and summed in bfloat16 or wider, within the bound.
A program may use at most 64 MiB of HBM per device.

```python
import math
import jax
import jax.numpy as jnp
from jax import lax

W = 1152
E = 1152
B_DEV = 128
GROUP_DEVS = 8
N = 4096


def steps_of(own_key, extent, shards, least, largest):
    level = 1.0
    for axis_at, parts in shards:
        steps = jax.random.uniform(jax.random.fold_in(jax.random.fold_in(own_key, 6), axis_at), (parts,), jnp.float32, least / len(shards), largest / len(shards))
        level = level * jnp.repeat(jnp.exp(steps), extent[axis_at] // parts).reshape((-1,) + (1,) * (len(extent) - 1 - axis_at))
    return level


def noise(stream_key, shape, scale, reach, split=(), kind=jnp.bfloat16):
    values = jax.random.normal(stream_key, shape, jnp.float32) * scale
    if len(split) > 0:
        values = steps_of(stream_key, shape, split, -0.22, 0.18) * values
    return jnp.clip(values, min=-reach, max=reach).astype(kind)


def setup_inputs(seed: int = 0) -> dict:
    key_of = jax.random.split(jax.random.key(seed), 7)
    image_feats = noise(key_of[0], (N, W), 1.0, 6.0, ((0, 32),))
    text_feats = noise(key_of[1], (N, W), 1.0, 6.0, ((0, 32),))
    image_proj = noise(key_of[2], (W, E), W ** -0.5, 0.1875)
    text_proj = noise(key_of[3], (W, E), W ** -0.5, 0.1875)
    scale = jnp.clip(jnp.exp(jax.random.uniform(key_of[4], (1,), jnp.float32, math.log(4.0), math.log(16.0))), 4.0, 16.0)
    bias = jnp.clip(jax.random.uniform(key_of[5], (1,), jnp.float32, -4.0, -2.0), -4.0, -2.0)
    return dict(image_feats=image_feats, text_feats=text_feats, image_proj=image_proj, text_proj=text_proj, scale=scale, bias=bias)


def project(feats, proj):
    raw_embed = jnp.dot(feats, proj, preferred_element_type=jnp.float32)
    recip = lax.rsqrt(lax.optimization_barrier(jnp.sum(raw_embed * raw_embed, axis=1, keepdims=True)) + 1e-06)
    unit = raw_embed * recip
    return (unit, recip, unit.astype(jnp.bfloat16))

def descend(unit, recip, grad_unit, proj):
    inner = lax.optimization_barrier(jnp.sum(unit * grad_unit, axis=1, keepdims=True))
    grad_raw = (recip * (grad_unit - unit * inner)).astype(jnp.bfloat16)
    return jnp.dot(grad_raw, proj.T, preferred_element_type=jnp.float32)

def reference(image_feats, text_feats, image_proj, text_proj, scale, bias):
    image_unit, image_recip, image_emb = project(image_feats, image_proj)
    text_unit, text_recip, text_emb = project(text_feats, text_proj)
    temper = scale[0]
    offset = bias[0]
    stride = N // (GROUP_DEVS * B_DEV)
    group_rows = GROUP_DEVS * B_DEV

    def regroup(values):
        return values.reshape(GROUP_DEVS, stride, B_DEV, E).transpose(1, 0, 2, 3).reshape(stride, group_rows, E)

    def ungroup(values):
        return values.reshape(stride, GROUP_DEVS, B_DEV, E).transpose(1, 0, 2, 3).reshape(N, E)
    matched = jnp.eye(group_rows, dtype=jnp.float32)

    def one_group(group_pair):
        image_rows, text_rows = group_pair
        logits = temper * jnp.dot(image_rows, text_rows.T, preferred_element_type=jnp.float32) + offset
        grad_logit = (jax.nn.sigmoid(logits) - matched).astype(jnp.bfloat16)
        image_part = jnp.dot(grad_logit, text_rows, preferred_element_type=jnp.float32)
        text_part = jnp.dot(grad_logit.T, image_rows, preferred_element_type=jnp.float32)
        return (image_part, text_part)
    image_parts, text_parts = lax.map(one_group, (regroup(image_emb), regroup(text_emb)))
    image_dz = temper * ungroup(image_parts)
    text_dz = temper * ungroup(text_parts)
    image_grad = descend(image_unit, image_recip, image_dz, image_proj)
    text_grad = descend(text_unit, text_recip, text_dz, text_proj)
    return (image_grad, text_grad)
```

```python
import functools

import jax
import jax.numpy as jnp
from jax import lax
from jax.experimental import pallas as pl
from jax.experimental.pallas import tpu as pltpu
from jax.sharding import PartitionSpec as P

GROUP_DEVS = 8
EARLY, LATE = 0, 1
OWN, SIB, AWAY, FAR = range(4)
RAW_PART = (1, 2)
LATE_PARTS = (2, 1, 1)
EARLY_BACK = (1, 1)
LATE_BACK = (2, 1, 1)


def flipped(member, bit):
    return member + bit - 2 * bit * lax.rem(lax.div(member, bit), 2)


def spans_of(rows, parts):
    total, at, out = sum(parts), 0, []
    for part in parts:
        size = rows * part // total
        out.append((at, size))
        at += size
    return out


def place_of(axis_sizes):
    hosts, locals_ = axis_sizes
    stride = hosts * locals_ // GROUP_DEVS
    position = lax.axis_index("hst") * locals_ + lax.axis_index("local")
    return lax.div(position, stride), lax.rem(position, stride), stride


def kernel(
    axis_sizes,
    image_feats,
    text_feats,
    image_proj,
    text_proj,
    scale,
    bias,
    done,
    last,
    late_proj_t,
    feats,
    away_feats,
    proj,
    early_proj_t,
    emb,
    unit,
    recip,
    own_sum,
    away_sum,
    away_out,
    away_in,
    temper_ref,
    offset_ref,
    load_sem,
    send_sem,
    recv_sem,
):
    member, rest, stride = place_of(axis_sizes)
    role = lax.rem(member, 2)
    locals_ = axis_sizes[1]

    def device_of(other):
        place = other * stride + rest
        return (lax.div(place, locals_), lax.rem(place, locals_))

    sibling = device_of(flipped(member, 1))
    image_partner = flipped(member, 2)
    text_partner = flipped(member, 4)
    partners = (
        device_of(text_partner * (1 - role) + image_partner * role),
        device_of(image_partner * (1 - role) + text_partner * role),
    )
    rows = image_feats.shape[0]

    def loads(early, late):
        copies = []
        for slot, (feat_ref, proj_ref) in enumerate((early, late)):
            copies.append(
                (
                    pltpu.make_async_copy(feat_ref, feats.at[slot], load_sem.at[slot, 0]),
                    pltpu.make_async_copy(proj_ref, proj.at[slot], load_sem.at[slot, 1]),
                )
            )
        return copies

    image, text = (image_feats, image_proj), (text_feats, text_proj)
    for which, (early, late) in enumerate(((text, image), (image, text))):

        @pl.when(role == which)
        def _():
            given = loads(early, late)
            for kind in range(2):
                for slot in range(2):
                    given[slot][kind].start()

    loaded = loads(image, text)
    knob_loads = [
        pltpu.make_async_copy(given, held, load_sem.at[2, i])
        for i, (given, held) in enumerate(((scale, temper_ref), (bias, offset_ref)))
    ]
    for copy in knob_loads:
        copy.start()

    barrier = pltpu.get_barrier_semaphore()
    for other in (sibling,) + partners:
        pl.semaphore_signal(
            barrier, inc=1, device_id=other, device_id_type=pl.DeviceIdType.MESH
        )

    copies = {}

    def send(name, src, dst, device):
        index = len(copies)
        copy = pltpu.make_async_remote_copy(
            src_ref=src,
            dst_ref=dst,
            send_sem=send_sem.at[index],
            recv_sem=recv_sem.at[index],
            device_id=device,
            device_id_type=pl.DeviceIdType.MESH,
        )
        copy.start()
        copies[name] = copy

    def embed(rows_in, side):
        raw = jnp.dot(rows_in, proj[side], preferred_element_type=jnp.float32)
        inverse = lax.rsqrt(jnp.sum(raw * raw, axis=1, keepdims=True) + 1e-06)
        return raw * inverse, inverse

    def embed_own(side):
        loaded[side][1].wait()
        normal, inverse = embed(feats[side], side)
        unit[side] = normal
        recip[side] = inverse
        emb[side, OWN] = normal.astype(jnp.bfloat16)

    raw_rows = rows * RAW_PART[0] // RAW_PART[1]
    raw_span, emb_span = pl.ds(0, raw_rows), pl.ds(raw_rows, rows - raw_rows)
    late_spans = [pl.ds(*s) for s in spans_of(rows, LATE_PARTS)]
    back_spans = [
        [pl.ds(*s) for s in spans_of(rows, parts)] for parts in (EARLY_BACK, LATE_BACK)
    ]
    whole = pl.ds(0, rows)

    loaded[EARLY][0].wait()
    loaded[LATE][0].wait()
    pl.semaphore_wait(barrier, 3)
    send("raw", feats.at[EARLY, raw_span], away_feats.at[raw_span], partners[EARLY])
    embed_own(EARLY)
    send(
        "early",
        emb.at[EARLY, OWN, emb_span],
        emb.at[EARLY, AWAY, emb_span],
        partners[EARLY],
    )
    send("sib early", emb.at[EARLY, OWN], emb.at[LATE, SIB], sibling)
    embed_own(LATE)
    for i, span in enumerate(late_spans):
        send(("late", i), emb.at[LATE, OWN, span], emb.at[LATE, AWAY, span], partners[LATE])
    send("sib late", emb.at[LATE, OWN], emb.at[EARLY, SIB], sibling)

    for copy in knob_loads:
        copy.wait()
    temper = temper_ref[0]
    offset = offset_ref[0]

    def pull(mine, theirs, own=False):
        logits = temper * lax.dot_general(
            mine, theirs, (((1,), (1,)), ((), ())), preferred_element_type=jnp.float32
        ) + offset
        slope = jax.nn.sigmoid(logits)
        if own:
            down = lax.broadcasted_iota(jnp.int32, slope.shape, 0)
            along = lax.broadcasted_iota(jnp.int32, slope.shape, 1)
            slope = slope - jnp.where(down == along, 1.0, 0.0)
        return jnp.dot(
            slope.astype(jnp.bfloat16), theirs, preferred_element_type=jnp.float32
        )

    def blocks(side, first, end):
        return emb[side, first:end].reshape((end - first) * rows, emb.shape[3])

    copies["sib early"].wait_recv()
    own_sum[EARLY] = pull(emb[EARLY, OWN], blocks(LATE, OWN, AWAY), own=True)
    copies["sib late"].wait_recv()
    own_sum[LATE] = pull(emb[LATE, OWN], blocks(EARLY, OWN, AWAY), own=True)

    copies["raw"].wait_recv()
    emb[EARLY, AWAY, raw_span] = embed(away_feats[raw_span], EARLY)[0].astype(jnp.bfloat16)
    send(
        "relay raw", emb.at[EARLY, AWAY, raw_span], emb.at[LATE, FAR, raw_span], sibling
    )
    copies["early"].wait_recv()
    send(
        "relay early", emb.at[EARLY, AWAY, emb_span], emb.at[LATE, FAR, emb_span], sibling
    )
    away_sum[EARLY] = pull(emb[EARLY, AWAY], blocks(LATE, OWN, AWAY))
    copies["relay raw"].wait_recv()
    copies["relay early"].wait_recv()
    away_sum[EARLY] += pull(emb[EARLY, AWAY], emb[LATE, FAR])

    for i, span in enumerate(late_spans):
        copies["late", i].wait_recv()
        send(("relay late", i), emb.at[LATE, AWAY, span], emb.at[EARLY, FAR, span], sibling)
        part = pull(emb[EARLY, AWAY], emb[LATE, AWAY, span])
        if i < len(late_spans) - 1:
            away_sum[EARLY] += part
        else:
            away_out[EARLY] = (away_sum[EARLY] + part).astype(jnp.bfloat16)
    for i, span in enumerate(back_spans[EARLY]):
        send(
            ("back", EARLY, i),
            away_out.at[EARLY, span],
            away_in.at[EARLY, span],
            partners[EARLY],
        )

    away_sum[LATE] = pull(emb[LATE, AWAY], blocks(EARLY, OWN, FAR))
    for i in range(len(late_spans)):
        copies["relay late", i].wait_recv()
    away_out[LATE] = (
        away_sum[LATE] + pull(emb[LATE, AWAY], emb[EARLY, FAR])
    ).astype(jnp.bfloat16)
    for i, span in enumerate(back_spans[LATE]):
        send(
            ("back", LATE, i), away_out.at[LATE, span], away_in.at[LATE, span], partners[LATE]
        )

    own_sum[EARLY] += pull(emb[EARLY, OWN], blocks(LATE, AWAY, FAR + 1))
    own_sum[LATE] += pull(emb[LATE, OWN], blocks(EARLY, AWAY, FAR + 1))
    early_proj_t[...] = proj[EARLY].T
    late_proj_t[...] = proj[LATE].T

    for side in range(2):
        for i, span in enumerate(back_spans[side]):
            copies["back", side, i].wait_recv()
            slope = temper * (own_sum[side, span] + away_in[side, span].astype(jnp.float32))
            normal = unit[side, span]
            inner = jnp.sum(normal * slope, axis=1, keepdims=True)
            down = (recip[side, span] * (slope - normal * inner)).astype(jnp.bfloat16)
            if side == LATE and i == len(back_spans[side]) - 1:
                last[...] = down
            else:
                done[side, span] = jnp.dot(
                    down,
                    (early_proj_t if side == EARLY else late_proj_t)[...],
                    preferred_element_type=jnp.float32,
                )

    for copy in copies.values():
        copy.wait_send()


def finish(axis_sizes, done, last, late_proj_t, image_grad, text_grad, tail, sem):
    role = lax.rem(place_of(axis_sizes)[0], 2)
    rows = done.shape[1]
    head, end = pl.ds(0, rows - last.shape[0]), pl.ds(rows - last.shape[0], last.shape[0])

    def puts(early_grad, late_grad):
        return (
            pltpu.make_async_copy(done.at[EARLY], early_grad, sem.at[0]),
            pltpu.make_async_copy(done.at[LATE, head], late_grad.at[head], sem.at[1]),
            pltpu.make_async_copy(tail, late_grad.at[end], sem.at[2]),
        )

    for which, grads in enumerate(((text_grad, image_grad), (image_grad, text_grad))):

        @pl.when(role == which)
        def _():
            for copy in puts(*grads)[:2]:
                copy.start()

    tail[...] = jnp.dot(last[...], late_proj_t[...], preferred_element_type=jnp.float32)
    for which, grads in enumerate(((text_grad, image_grad), (image_grad, text_grad))):

        @pl.when(role == which)
        def _():
            puts(*grads)[2].start()

    for copy in puts(text_grad, image_grad):
        copy.wait()


def on_device(axis_sizes, image_feats, text_feats, image_proj, text_proj, scale, bias):
    rows, width = image_feats.shape
    embed = image_proj.shape[1]
    f32, bf16 = jnp.float32, jnp.bfloat16
    hbm = pl.BlockSpec(memory_space=pltpu.HBM)
    vmem = pl.BlockSpec(memory_space=pltpu.VMEM)
    end = spans_of(rows, LATE_BACK)[-1][1]
    n_copies = 6 + 2 * len(LATE_PARTS) + len(EARLY_BACK) + len(LATE_BACK)
    done, last, late_proj_t = pl.pallas_call(
        functools.partial(kernel, axis_sizes),
        out_shape=(
            pltpu.VMEM((2, rows, width), f32),
            pltpu.VMEM((end, embed), bf16),
            pltpu.VMEM((embed, width), bf16),
        ),
        in_specs=[hbm] * 6,
        out_specs=(vmem,) * 3,
        scratch_shapes=[
            pltpu.VMEM((2, rows, width), bf16),
            pltpu.VMEM((rows, width), bf16),
            pltpu.VMEM((2, width, embed), bf16),
            pltpu.VMEM((embed, width), bf16),
            pltpu.VMEM((2, 4, rows, embed), bf16),
            pltpu.VMEM((2, rows, embed), f32),
            pltpu.VMEM((2, rows, 1), f32),
            pltpu.VMEM((2, rows, embed), f32),
            pltpu.VMEM((2, rows, embed), f32),
            pltpu.VMEM((2, rows, embed), bf16),
            pltpu.VMEM((2, rows, embed), bf16),
            pltpu.SMEM((1,), f32),
            pltpu.SMEM((1,), f32),
            pltpu.SemaphoreType.DMA((3, 2)),
            pltpu.SemaphoreType.DMA((n_copies,)),
            pltpu.SemaphoreType.DMA((n_copies,)),
        ],
        compiler_params=pltpu.CompilerParams(
            collective_id=0, has_side_effects=True, vmem_limit_bytes=36700160
        ),
    )(
        *(
            pltpu.with_memory_space_constraint(x, pltpu.HBM)
            for x in (image_feats, text_feats, image_proj, text_proj)
        ),
        scale,
        bias,
    )
    out = jax.ShapeDtypeStruct((rows, width), f32)
    return pl.pallas_call(
        functools.partial(finish, axis_sizes),
        out_shape=(out, out),
        in_specs=[vmem] * 3,
        out_specs=(hbm, hbm),
        scratch_shapes=[
            pltpu.VMEM((end, width), f32),
            pltpu.SemaphoreType.DMA((3,)),
        ],
        compiler_params=pltpu.CompilerParams(vmem_limit_bytes=8388608),
    )(*(pltpu.with_memory_space_constraint(x, pltpu.VMEM) for x in (done, last, late_proj_t)))


def solution(mesh):
    in_specs = (P(("hst", "local"), None), P(("hst", "local"), None), P(), P(), P(), P())
    out_specs = (P(("hst", "local"), None), P(("hst", "local"), None))
    axis_sizes = (mesh.shape["hst"], mesh.shape["local"])
    return jax.shard_map(
        functools.partial(on_device, axis_sizes),
        mesh=mesh,
        in_specs=in_specs,
        out_specs=out_specs,
        check_vma=False,
    )
```

```python
import functools

import jax
import jax.numpy as jnp
from jax import lax
from jax.experimental import pallas as pl
from jax.experimental.pallas import tpu as pltpu
from jax.sharding import PartitionSpec as P

GROUP_DEVS = 8
EARLY, LATE = 0, 1
OWN, SIB, FAR, AWAY = range(4)
RAW_PART = (1, 2)
LATE_PARTS = (2, 1, 1)
EARLY_BACK = (1, 1)
LATE_BACK = (3, 1)


def flipped(member, bit):
    return member + bit - 2 * bit * lax.rem(lax.div(member, bit), 2)


def spans_of(rows, parts):
    total, at, out = sum(parts), 0, []
    for part in parts:
        size = rows * part // total
        out.append((at, size))
        at += size
    return out


def place_of(axis_sizes):
    hosts, locals_ = axis_sizes
    stride = hosts * locals_ // GROUP_DEVS
    position = lax.axis_index("hst") * locals_ + lax.axis_index("local")
    return lax.div(position, stride), lax.rem(position, stride), stride


def kernel(
    axis_sizes,
    image_feats,
    text_feats,
    image_proj,
    text_proj,
    scale,
    bias,
    done,
    last,
    late_proj_t,
    feats,
    away_feats,
    proj,
    early_proj_t,
    emb,
    unit,
    recip,
    own_sum,
    away_sum,
    away_out,
    away_in,
    temper_ref,
    offset_ref,
    load_sem,
    send_sem,
    recv_sem,
):
    member, rest, stride = place_of(axis_sizes)
    role = lax.rem(member, 2)
    locals_ = axis_sizes[1]

    def device_of(other):
        place = other * stride + rest
        return (lax.div(place, locals_), lax.rem(place, locals_))

    sibling = device_of(flipped(member, 1))
    image_partner = flipped(member, 2)
    text_partner = flipped(member, 4)
    partners = (
        device_of(text_partner * (1 - role) + image_partner * role),
        device_of(image_partner * (1 - role) + text_partner * role),
    )
    rows = image_feats.shape[0]

    def loads(early, late):
        copies = []
        for slot, (feat_ref, proj_ref) in enumerate((early, late)):
            copies.append(
                (
                    pltpu.make_async_copy(feat_ref, feats.at[slot], load_sem.at[slot, 0]),
                    pltpu.make_async_copy(proj_ref, proj.at[slot], load_sem.at[slot, 1]),
                )
            )
        return copies

    image, text = (image_feats, image_proj), (text_feats, text_proj)
    for which, (early, late) in enumerate(((text, image), (image, text))):

        @pl.when(role == which)
        def _():
            given = loads(early, late)
            for kind in range(2):
                for slot in range(2):
                    given[slot][kind].start()

    loaded = loads(image, text)
    knob_loads = [
        pltpu.make_async_copy(given, held, load_sem.at[2, i])
        for i, (given, held) in enumerate(((scale, temper_ref), (bias, offset_ref)))
    ]
    for copy in knob_loads:
        copy.start()

    barrier = pltpu.get_barrier_semaphore()
    for other in (sibling,) + partners:
        pl.semaphore_signal(
            barrier, inc=1, device_id=other, device_id_type=pl.DeviceIdType.MESH
        )

    copies = {}

    def send(name, src, dst, device):
        index = len(copies)
        copy = pltpu.make_async_remote_copy(
            src_ref=src,
            dst_ref=dst,
            send_sem=send_sem.at[index],
            recv_sem=recv_sem.at[index],
            device_id=device,
            device_id_type=pl.DeviceIdType.MESH,
        )
        copy.start()
        copies[name] = copy

    def embed(rows_in, side):
        raw = jnp.dot(rows_in, proj[side], preferred_element_type=jnp.float32)
        inverse = lax.rsqrt(jnp.sum(raw * raw, axis=1, keepdims=True) + 1e-06)
        return raw * inverse, inverse

    def embed_own(side):
        loaded[side][1].wait()
        normal, inverse = embed(feats[side], side)
        unit[side] = normal
        recip[side] = inverse
        emb[side, OWN] = normal.astype(jnp.bfloat16)

    raw_rows = rows * RAW_PART[0] // RAW_PART[1]
    raw_span, emb_span = pl.ds(0, raw_rows), pl.ds(raw_rows, rows - raw_rows)
    late_spans = [pl.ds(*s) for s in spans_of(rows, LATE_PARTS)]
    back_spans = [
        [pl.ds(*s) for s in spans_of(rows, parts)] for parts in (EARLY_BACK, LATE_BACK)
    ]
    whole = pl.ds(0, rows)

    loaded[EARLY][0].wait()
    loaded[LATE][0].wait()
    pl.semaphore_wait(barrier, 3)
    send("raw", feats.at[EARLY, raw_span], away_feats.at[raw_span], partners[EARLY])
    embed_own(EARLY)
    send(
        "early",
        emb.at[EARLY, OWN, emb_span],
        emb.at[EARLY, AWAY, emb_span],
        partners[EARLY],
    )
    send("sib early", emb.at[EARLY, OWN], emb.at[LATE, SIB], sibling)
    embed_own(LATE)
    for i, span in enumerate(late_spans):
        send(("late", i), emb.at[LATE, OWN, span], emb.at[LATE, AWAY, span], partners[LATE])
    send("sib late", emb.at[LATE, OWN], emb.at[EARLY, SIB], sibling)

    for copy in knob_loads:
        copy.wait()
    temper = temper_ref[0]
    offset = offset_ref[0]

    def pull(mine, theirs, own=False):
        logits = temper * lax.dot_general(
            mine, theirs, (((1,), (1,)), ((), ())), preferred_element_type=jnp.float32
        ) + offset
        slope = jax.nn.sigmoid(logits)
        if own:
            down = lax.broadcasted_iota(jnp.int32, slope.shape, 0)
            along = lax.broadcasted_iota(jnp.int32, slope.shape, 1)
            slope = slope - jnp.where(down == along, 1.0, 0.0)
        return jnp.dot(
            slope.astype(jnp.bfloat16), theirs, preferred_element_type=jnp.float32
        )

    def blocks(side, first, end):
        return emb[side, first:end].reshape((end - first) * rows, emb.shape[3])

    copies["sib early"].wait_recv()
    own_sum[EARLY] = pull(emb[EARLY, OWN], blocks(LATE, OWN, FAR), own=True)
    copies["sib late"].wait_recv()
    own_sum[LATE] = pull(emb[LATE, OWN], blocks(EARLY, OWN, FAR), own=True)

    copies["raw"].wait_recv()
    emb[EARLY, AWAY, raw_span] = embed(away_feats[raw_span], EARLY)[0].astype(jnp.bfloat16)
    send(
        "relay raw", emb.at[EARLY, AWAY, raw_span], emb.at[LATE, FAR, raw_span], sibling
    )
    copies["early"].wait_recv()
    send(
        "relay early", emb.at[EARLY, AWAY, emb_span], emb.at[LATE, FAR, emb_span], sibling
    )
    away_sum[...] = pull(emb[EARLY, AWAY], blocks(LATE, OWN, FAR))
    for i, span in enumerate(late_spans):
        copies["late", i].wait_recv()
        send(("relay late", i), emb.at[LATE, AWAY, span], emb.at[EARLY, FAR, span], sibling)
    copies["relay raw"].wait_recv()
    copies["relay early"].wait_recv()
    away_out[EARLY] = (
        away_sum[...] + pull(emb[EARLY, AWAY], blocks(LATE, FAR, AWAY + 1))
    ).astype(jnp.bfloat16)
    for i, span in enumerate(back_spans[EARLY]):
        send(
            ("back", EARLY, i),
            away_out.at[EARLY, span],
            away_in.at[EARLY, span],
            partners[EARLY],
        )

    for i in range(len(late_spans)):
        copies["relay late", i].wait_recv()
    away_out[LATE] = pull(emb[LATE, AWAY], blocks(EARLY, OWN, AWAY + 1)).astype(jnp.bfloat16)
    for i, span in enumerate(back_spans[LATE]):
        send(
            ("back", LATE, i), away_out.at[LATE, span], away_in.at[LATE, span], partners[LATE]
        )

    own_sum[EARLY] += pull(emb[EARLY, OWN], blocks(LATE, FAR, AWAY + 1))
    own_sum[LATE] += pull(emb[LATE, OWN], blocks(EARLY, FAR, AWAY + 1))
    early_proj_t[...] = proj[EARLY].T
    late_proj_t[...] = proj[LATE].T

    def down_of(side, span):
        slope = temper * (own_sum[side, span] + away_in[side, span].astype(jnp.float32))
        normal = unit[side, span]
        inner = jnp.sum(normal * slope, axis=1, keepdims=True)
        return (recip[side, span] * (slope - normal * inner)).astype(jnp.bfloat16)

    for i in range(len(back_spans[EARLY])):
        copies["back", EARLY, i].wait_recv()
    done[EARLY] = jnp.dot(
        down_of(EARLY, whole), early_proj_t[...], preferred_element_type=jnp.float32
    )
    for i, span in enumerate(back_spans[LATE]):
        copies["back", LATE, i].wait_recv()
        down = down_of(LATE, span)
        if i < len(back_spans[LATE]) - 1:
            done[LATE, span] = jnp.dot(
                down, late_proj_t[...], preferred_element_type=jnp.float32
            )
        else:
            last[...] = down

    for copy in copies.values():
        copy.wait_send()


def finish(axis_sizes, done, last, late_proj_t, image_grad, text_grad, tail, sem):
    role = lax.rem(place_of(axis_sizes)[0], 2)
    rows = done.shape[1]
    head, end = pl.ds(0, rows - last.shape[0]), pl.ds(rows - last.shape[0], last.shape[0])

    def puts(early_grad, late_grad):
        return (
            pltpu.make_async_copy(done.at[EARLY], early_grad, sem.at[0]),
            pltpu.make_async_copy(done.at[LATE, head], late_grad.at[head], sem.at[1]),
            pltpu.make_async_copy(tail, late_grad.at[end], sem.at[2]),
        )

    for which, grads in enumerate(((text_grad, image_grad), (image_grad, text_grad))):

        @pl.when(role == which)
        def _():
            for copy in puts(*grads)[:2]:
                copy.start()

    @pl.when(role >= 0)
    def _():
        tail[...] = jnp.dot(last[...], late_proj_t[...], preferred_element_type=jnp.float32)

    for which, grads in enumerate(((text_grad, image_grad), (image_grad, text_grad))):

        @pl.when(role == which)
        def _():
            puts(*grads)[2].start()

    for copy in puts(text_grad, image_grad):
        copy.wait()


def on_device(axis_sizes, image_feats, text_feats, image_proj, text_proj, scale, bias):
    rows, width = image_feats.shape
    embed = image_proj.shape[1]
    f32, bf16 = jnp.float32, jnp.bfloat16
    hbm = pl.BlockSpec(memory_space=pltpu.HBM)
    vmem = pl.BlockSpec(memory_space=pltpu.VMEM)
    end = spans_of(rows, LATE_BACK)[-1][1]
    n_copies = 6 + 2 * len(LATE_PARTS) + len(EARLY_BACK) + len(LATE_BACK)
    done, last, late_proj_t = pl.pallas_call(
        functools.partial(kernel, axis_sizes),
        out_shape=(
            pltpu.VMEM((2, rows, width), f32),
            pltpu.VMEM((end, embed), bf16),
            pltpu.VMEM((embed, width), bf16),
        ),
        in_specs=[hbm] * 6,
        out_specs=(vmem,) * 3,
        scratch_shapes=[
            pltpu.VMEM((2, rows, width), bf16),
            pltpu.VMEM((rows, width), bf16),
            pltpu.VMEM((2, width, embed), bf16),
            pltpu.VMEM((embed, width), bf16),
            pltpu.VMEM((2, 4, rows, embed), bf16),
            pltpu.VMEM((2, rows, embed), f32),
            pltpu.VMEM((2, rows, 1), f32),
            pltpu.VMEM((2, rows, embed), f32),
            pltpu.VMEM((rows, embed), f32),
            pltpu.VMEM((2, rows, embed), bf16),
            pltpu.VMEM((2, rows, embed), bf16),
            pltpu.SMEM((1,), f32),
            pltpu.SMEM((1,), f32),
            pltpu.SemaphoreType.DMA((3, 2)),
            pltpu.SemaphoreType.DMA((n_copies,)),
            pltpu.SemaphoreType.DMA((n_copies,)),
        ],
        compiler_params=pltpu.CompilerParams(
            collective_id=0, has_side_effects=True, vmem_limit_bytes=36700160
        ),
    )(
        *(
            pltpu.with_memory_space_constraint(x, pltpu.HBM)
            for x in (image_feats, text_feats, image_proj, text_proj)
        ),
        scale,
        bias,
    )
    out = jax.ShapeDtypeStruct((rows, width), f32)
    return pl.pallas_call(
        functools.partial(finish, axis_sizes),
        out_shape=(out, out),
        in_specs=[vmem] * 3,
        out_specs=(hbm, hbm),
        scratch_shapes=[
            pltpu.VMEM((end, width), f32),
            pltpu.SemaphoreType.DMA((3,)),
        ],
        compiler_params=pltpu.CompilerParams(vmem_limit_bytes=8388608),
    )(*(pltpu.with_memory_space_constraint(x, pltpu.VMEM) for x in (done, last, late_proj_t)))


def solution(mesh):
    in_specs = (P(("hst", "local"), None), P(("hst", "local"), None), P(), P(), P(), P())
    out_specs = (P(("hst", "local"), None), P(("hst", "local"), None))
    axis_sizes = (mesh.shape["hst"], mesh.shape["local"])
    return jax.shard_map(
        functools.partial(on_device, axis_sizes),
        mesh=mesh,
        in_specs=in_specs,
        out_specs=out_specs,
        check_vma=False,
    )
```

```python
import functools

import jax
import jax.numpy as jnp
from jax import lax
from jax.experimental import pallas as pl
from jax.experimental.pallas import tpu as pltpu
from jax.sharding import PartitionSpec as P

GROUP_DEVS = 8
EARLY, LATE = 0, 1
OWN, SIB, FAR, AWAY = range(4)
RAW_PART = (1, 2)
LATE_PARTS = (2, 1, 1)
EARLY_BACK = (1, 1)
LATE_BACK = (3, 1)


def flipped(member, bit):
    return member + bit - 2 * bit * lax.rem(lax.div(member, bit), 2)


def spans_of(rows, parts):
    total, at, out = sum(parts), 0, []
    for part in parts:
        size = rows * part // total
        out.append((at, size))
        at += size
    return out


def place_of(axis_sizes):
    hosts, locals_ = axis_sizes
    stride = hosts * locals_ // GROUP_DEVS
    position = lax.axis_index("hst") * locals_ + lax.axis_index("local")
    return lax.div(position, stride), lax.rem(position, stride), stride


def kernel(
    axis_sizes,
    image_feats,
    text_feats,
    image_proj,
    text_proj,
    scale,
    bias,
    done,
    last,
    late_proj_t,
    feats,
    away_feats,
    proj,
    early_proj_t,
    emb,
    unit,
    recip,
    own_sum,
    away_sum,
    away_out,
    away_in,
    temper_ref,
    offset_ref,
    load_sem,
    send_sem,
    recv_sem,
):
    member, rest, stride = place_of(axis_sizes)
    role = lax.rem(member, 2)
    locals_ = axis_sizes[1]

    def device_of(other):
        place = other * stride + rest
        return (lax.div(place, locals_), lax.rem(place, locals_))

    sibling = device_of(flipped(member, 1))
    image_partner = flipped(member, 2)
    text_partner = flipped(member, 4)
    partners = (
        device_of(text_partner * (1 - role) + image_partner * role),
        device_of(image_partner * (1 - role) + text_partner * role),
    )
    rows = image_feats.shape[0]

    def loads(early, late):
        copies = []
        for slot, (feat_ref, proj_ref) in enumerate((early, late)):
            copies.append(
                (
                    pltpu.make_async_copy(feat_ref, feats.at[slot], load_sem.at[slot, 0]),
                    pltpu.make_async_copy(proj_ref, proj.at[slot], load_sem.at[slot, 1]),
                )
            )
        return copies

    image, text = (image_feats, image_proj), (text_feats, text_proj)
    for which, (early, late) in enumerate(((text, image), (image, text))):

        @pl.when(role == which)
        def _():
            given = loads(early, late)
            for kind in range(2):
                for slot in range(2):
                    given[slot][kind].start()

    loaded = loads(image, text)
    knob_loads = [
        pltpu.make_async_copy(given, held, load_sem.at[2, i])
        for i, (given, held) in enumerate(((scale, temper_ref), (bias, offset_ref)))
    ]
    for copy in knob_loads:
        copy.start()

    barrier = pltpu.get_barrier_semaphore()
    for other in (sibling,) + partners:
        pl.semaphore_signal(
            barrier, inc=1, device_id=other, device_id_type=pl.DeviceIdType.MESH
        )

    copies = {}

    def send(name, src, dst, device):
        index = len(copies)
        copy = pltpu.make_async_remote_copy(
            src_ref=src,
            dst_ref=dst,
            send_sem=send_sem.at[index],
            recv_sem=recv_sem.at[index],
            device_id=device,
            device_id_type=pl.DeviceIdType.MESH,
        )
        copy.start()
        copies[name] = copy

    def embed(rows_in, side):
        raw = jnp.dot(rows_in, proj[side], preferred_element_type=jnp.float32)
        inverse = lax.rsqrt(jnp.sum(raw * raw, axis=1, keepdims=True) + 1e-06)
        return raw * inverse, inverse

    def embed_own(side):
        loaded[side][1].wait()
        normal, inverse = embed(feats[side], side)
        unit[side] = normal
        recip[side] = inverse
        emb[side, OWN] = normal.astype(jnp.bfloat16)

    raw_rows = rows * RAW_PART[0] // RAW_PART[1]
    raw_span, emb_span = pl.ds(0, raw_rows), pl.ds(raw_rows, rows - raw_rows)
    late_spans = [pl.ds(*s) for s in spans_of(rows, LATE_PARTS)]
    back_spans = [
        [pl.ds(*s) for s in spans_of(rows, parts)] for parts in (EARLY_BACK, LATE_BACK)
    ]
    whole = pl.ds(0, rows)

    loaded[EARLY][0].wait()
    loaded[LATE][0].wait()
    pl.semaphore_wait(barrier, 3)
    send("raw", feats.at[EARLY, raw_span], away_feats.at[raw_span], partners[EARLY])
    embed_own(EARLY)
    send(
        "early",
        emb.at[EARLY, OWN, emb_span],
        emb.at[EARLY, AWAY, emb_span],
        partners[EARLY],
    )
    send("sib early", emb.at[EARLY, OWN], emb.at[LATE, SIB], sibling)
    embed_own(LATE)
    for i, span in enumerate(late_spans):
        send(("late", i), emb.at[LATE, OWN, span], emb.at[LATE, AWAY, span], partners[LATE])
    send("sib late", emb.at[LATE, OWN], emb.at[EARLY, SIB], sibling)

    for copy in knob_loads:
        copy.wait()
    temper = temper_ref[0]
    offset = offset_ref[0]

    def pull(mine, theirs, own=False):
        logits = temper * lax.dot_general(
            mine, theirs, (((1,), (1,)), ((), ())), preferred_element_type=jnp.float32
        ) + offset
        slope = jax.nn.sigmoid(logits)
        if own:
            down = lax.broadcasted_iota(jnp.int32, slope.shape, 0)
            along = lax.broadcasted_iota(jnp.int32, slope.shape, 1)
            slope = slope - jnp.where(down == along, 1.0, 0.0)
        return jnp.dot(
            slope.astype(jnp.bfloat16), theirs, preferred_element_type=jnp.float32
        )

    def blocks(side, first, end):
        return emb[side, first:end].reshape((end - first) * rows, emb.shape[3])

    copies["raw"].wait_recv()
    emb[EARLY, AWAY, raw_span] = embed(away_feats[raw_span], EARLY)[0].astype(jnp.bfloat16)
    send(
        "relay raw", emb.at[EARLY, AWAY, raw_span], emb.at[LATE, FAR, raw_span], sibling
    )
    copies["early"].wait_recv()
    send(
        "relay early", emb.at[EARLY, AWAY, emb_span], emb.at[LATE, FAR, emb_span], sibling
    )
    copies["sib early"].wait_recv()
    away_sum[...] = pull(emb[EARLY, AWAY], blocks(LATE, OWN, FAR))
    for i, span in enumerate(late_spans):
        copies["late", i].wait_recv()
        send(("relay late", i), emb.at[LATE, AWAY, span], emb.at[EARLY, FAR, span], sibling)
    copies["relay raw"].wait_recv()
    copies["relay early"].wait_recv()
    away_out[EARLY] = (
        away_sum[...] + pull(emb[EARLY, AWAY], blocks(LATE, FAR, AWAY + 1))
    ).astype(jnp.bfloat16)
    for i, span in enumerate(back_spans[EARLY]):
        send(
            ("back", EARLY, i),
            away_out.at[EARLY, span],
            away_in.at[EARLY, span],
            partners[EARLY],
        )

    copies["sib late"].wait_recv()
    for i in range(len(late_spans)):
        copies["relay late", i].wait_recv()
    away_out[LATE] = pull(emb[LATE, AWAY], blocks(EARLY, OWN, AWAY + 1)).astype(jnp.bfloat16)
    for i, span in enumerate(back_spans[LATE]):
        send(
            ("back", LATE, i), away_out.at[LATE, span], away_in.at[LATE, span], partners[LATE]
        )

    for side in range(2):
        own_sum[side] = pull(emb[side, OWN], blocks(1 - side, OWN, AWAY + 1), own=True)
    early_proj_t[...] = proj[EARLY].T
    late_proj_t[...] = proj[LATE].T

    def down_of(side, span):
        slope = temper * (own_sum[side, span] + away_in[side, span].astype(jnp.float32))
        normal = unit[side, span]
        inner = jnp.sum(normal * slope, axis=1, keepdims=True)
        return (recip[side, span] * (slope - normal * inner)).astype(jnp.bfloat16)

    for i in range(len(back_spans[EARLY])):
        copies["back", EARLY, i].wait_recv()
    done[EARLY] = jnp.dot(
        down_of(EARLY, whole), early_proj_t[...], preferred_element_type=jnp.float32
    )
    for i, span in enumerate(back_spans[LATE]):
        copies["back", LATE, i].wait_recv()
        down = down_of(LATE, span)
        if i < len(back_spans[LATE]) - 1:
            done[LATE, span] = jnp.dot(
                down, late_proj_t[...], preferred_element_type=jnp.float32
            )
        else:
            last[...] = down

    for copy in copies.values():
        copy.wait_send()


def finish(axis_sizes, done, last, late_proj_t, image_grad, text_grad, tail, sem):
    role = lax.rem(place_of(axis_sizes)[0], 2)
    rows = done.shape[1]
    head, end = pl.ds(0, rows - last.shape[0]), pl.ds(rows - last.shape[0], last.shape[0])

    def puts(early_grad, late_grad):
        return (
            pltpu.make_async_copy(done.at[EARLY], early_grad, sem.at[0]),
            pltpu.make_async_copy(done.at[LATE, head], late_grad.at[head], sem.at[1]),
            pltpu.make_async_copy(tail, late_grad.at[end], sem.at[2]),
        )

    for which, grads in enumerate(((text_grad, image_grad), (image_grad, text_grad))):

        @pl.when(role == which)
        def _():
            for copy in puts(*grads)[:2]:
                copy.start()

    @pl.when(role >= 0)
    def _():
        tail[...] = jnp.dot(last[...], late_proj_t[...], preferred_element_type=jnp.float32)

    for which, grads in enumerate(((text_grad, image_grad), (image_grad, text_grad))):

        @pl.when(role == which)
        def _():
            puts(*grads)[2].start()

    for copy in puts(text_grad, image_grad):
        copy.wait()


def on_device(axis_sizes, image_feats, text_feats, image_proj, text_proj, scale, bias):
    rows, width = image_feats.shape
    embed = image_proj.shape[1]
    f32, bf16 = jnp.float32, jnp.bfloat16
    hbm = pl.BlockSpec(memory_space=pltpu.HBM)
    vmem = pl.BlockSpec(memory_space=pltpu.VMEM)
    end = spans_of(rows, LATE_BACK)[-1][1]
    n_copies = 6 + 2 * len(LATE_PARTS) + len(EARLY_BACK) + len(LATE_BACK)
    done, last, late_proj_t = pl.pallas_call(
        functools.partial(kernel, axis_sizes),
        out_shape=(
            pltpu.VMEM((2, rows, width), f32),
            pltpu.VMEM((end, embed), bf16),
            pltpu.VMEM((embed, width), bf16),
        ),
        in_specs=[hbm] * 6,
        out_specs=(vmem,) * 3,
        scratch_shapes=[
            pltpu.VMEM((2, rows, width), bf16),
            pltpu.VMEM((rows, width), bf16),
            pltpu.VMEM((2, width, embed), bf16),
            pltpu.VMEM((embed, width), bf16),
            pltpu.VMEM((2, 4, rows, embed), bf16),
            pltpu.VMEM((2, rows, embed), f32),
            pltpu.VMEM((2, rows, 1), f32),
            pltpu.VMEM((2, rows, embed), f32),
            pltpu.VMEM((rows, embed), f32),
            pltpu.VMEM((2, rows, embed), bf16),
            pltpu.VMEM((2, rows, embed), bf16),
            pltpu.SMEM((1,), f32),
            pltpu.SMEM((1,), f32),
            pltpu.SemaphoreType.DMA((3, 2)),
            pltpu.SemaphoreType.DMA((n_copies,)),
            pltpu.SemaphoreType.DMA((n_copies,)),
        ],
        compiler_params=pltpu.CompilerParams(
            collective_id=0, has_side_effects=True, vmem_limit_bytes=36700160
        ),
    )(
        *(
            pltpu.with_memory_space_constraint(x, pltpu.HBM)
            for x in (image_feats, text_feats, image_proj, text_proj)
        ),
        scale,
        bias,
    )
    out = jax.ShapeDtypeStruct((rows, width), f32)
    return pl.pallas_call(
        functools.partial(finish, axis_sizes),
        out_shape=(out, out),
        in_specs=[vmem] * 3,
        out_specs=(hbm, hbm),
        scratch_shapes=[
            pltpu.VMEM((end, width), f32),
            pltpu.SemaphoreType.DMA((3,)),
        ],
        compiler_params=pltpu.CompilerParams(vmem_limit_bytes=8388608),
    )(*(pltpu.with_memory_space_constraint(x, pltpu.VMEM) for x in (done, last, late_proj_t)))


def solution(mesh):
    in_specs = (P(("hst", "local"), None), P(("hst", "local"), None), P(), P(), P(), P())
    out_specs = (P(("hst", "local"), None), P(("hst", "local"), None))
    axis_sizes = (mesh.shape["hst"], mesh.shape["local"])
    return jax.shard_map(
        functools.partial(on_device, axis_sizes),
        mesh=mesh,
        in_specs=in_specs,
        out_specs=out_specs,
        check_vma=False,
    )
```
